32 devices in a mesh: grp: 2 (over x), blk: 16 (over z, y, core).
Axes of the slice: x: 2, y: 2, z: 4, core: 2. Of those that a mesh axis runs over, the one named last changes fastest.
Arguments:
- e_field: float32 [3, 128, 64, 128], P(None, 'blk', 'grp'), may hold values from -6 to 6
- h_field: float32 [3, 128, 64, 128], P(None, 'blk', 'grp'), may hold values from -6 to 6
- inv_eps: float32 [128, 64, 128], P('blk', 'grp'), may hold values from 0.08 to 1
- cot_e: float32 [3, 128, 64, 128], P(None, 'blk', 'grp'), may hold values from -6 to 6
- cot_h: float32 [3, 128, 64, 128], P(None, 'blk', 'grp'), may hold values from -6 to 6
- voxel_ids: int32 [128, 64, 128], P('blk', 'grp'), may hold values from 0 to 2047
Outputs:
- e_final: float32 [3, 128, 64, 128], P(None, 'blk', 'grp')
- h_final: float32 [3, 128, 64, 128], P(None, 'blk', 'grp')
- voxel_grad: float32 [2048], P(('grp', 'blk'))
The draws below stay inside these ranges and needn't reach their ends.
All inputs are finite; a program needn't handle non-finite values.
Results may differ from the reference program's by a relative error of at most 0.0001.
Values sent between devices are 32-bit elements; how exact they have to be, the bound alone decides.
A program may use at most 64 MiB of HBM per device.

```python
import math
import jax
import jax.numpy as jnp

NY = 128
STEPS = 4
NX = 128
NZ = 64
VOX = 2048


def plant(result, stream_key, least, largest):
    longest = result.shape.index(max(result.shape))
    spots = []
    for shift in (0, 1):
        where = [jax.random.randint(jax.random.fold_in(stream_key, axis), (), 0, length) for axis, length in enumerate(result.shape)]
        where[longest] = (where[longest] + shift) % result.shape[longest]
        spots.append(tuple(where))
    return result.at[spots[0]].set(least).at[spots[1]].set(largest)


def level_of(own_key, extent, cuts, low, top_value):
    factor_of, own = 1.0, jax.random.fold_in(own_key, 6)
    for axis_at, shards_of in cuts:
        heights = jnp.exp(jax.random.uniform(jax.random.fold_in(own, axis_at), (shards_of,), jnp.float32, low / len(cuts), top_value / len(cuts)))
        factor_of = factor_of * jnp.repeat(heights, extent[axis_at] // shards_of).reshape([-1 if axis == axis_at else 1 for axis in range(len(extent))])
    return factor_of


def noise(stream_key, dims, deviation, most, shards=(), dtype=jnp.bfloat16):
    gain = level_of(stream_key, dims, shards, -0.22, 0.18) if shards else 1.0
    drawn = jax.random.normal(stream_key, dims, jnp.float32) * deviation * gain
    return jnp.minimum(jnp.maximum(drawn, -most), most).astype(dtype)


def setup_inputs(seed: int = 0) -> dict:
    key_of = jax.random.split(jax.random.key(seed), 7)
    return {
        "e_field": noise(key_of[0], (3, NX, NZ, NY), 1.0, 6.0, ((1, 16), (2, 2)), jnp.float32),
        "h_field": noise(key_of[1], (3, NX, NZ, NY), 1.0, 6.0, ((1, 16), (2, 2)), jnp.float32),
        "inv_eps": jnp.clip(jnp.exp(math.log(1.0) - 2.5257287 * jax.random.uniform(key_of[2], (NX, NZ, NY), jnp.float32) ** level_of(key_of[2], (NX, NZ, NY), ((0, 16), (1, 2)), -0.2, 0.2)), 0.08, 1.0),
        "cot_e": noise(key_of[3], (3, NX, NZ, NY), 1.0, 6.0, ((1, 16), (2, 2)), jnp.float32),
        "cot_h": noise(key_of[4], (3, NX, NZ, NY), 1.0, 6.0, ((1, 16), (2, 2)), jnp.float32),
        "voxel_ids": plant(jax.random.randint(key_of[5], (NX, NZ, NY), 0, VOX), jax.random.fold_in(key_of[5], 1), 0, VOX - 1).astype(jnp.int32),
    }


courant = 0.5


def lax_slice(v, axis, start, stop):
    index = [slice(None)] * v.ndim
    index[axis] = slice(start, stop)
    return v[tuple(index)]


def diff_fwd(v, axis):
    size = v.shape[axis]
    upper = jnp.concatenate([lax_slice(v, axis, 1, size), jnp.zeros_like(lax_slice(v, axis, 0, 1))], axis=axis)
    return upper - v


def diff_bwd(v, axis):
    size = v.shape[axis]
    lower = jnp.concatenate([jnp.zeros_like(lax_slice(v, axis, 0, 1)), lax_slice(v, axis, 0, size - 1)], axis=axis)
    return v - lower


def curl_with(v, diff):
    vx, vy, vz = v[0], v[1], v[2]
    cx = diff(vz, 2) - diff(vy, 1)
    cy = diff(vx, 1) - diff(vz, 0)
    cz = diff(vy, 0) - diff(vx, 2)
    return jnp.stack([cx, cy, cz])


def reference(e_field, h_field, inv_eps, cot_e, cot_h, voxel_ids):
    curls = []
    for step in range(STEPS):
        h_field = h_field - courant * curl_with(e_field, diff_fwd)
        curl_now = curl_with(h_field, diff_bwd)
        curls.append(curl_now)
        e_field = e_field + courant * inv_eps[None] * curl_now
    adj_e, adj_h = cot_e, cot_h
    grad = jnp.zeros(inv_eps.shape, jnp.float32)
    for step in range(STEPS - 1, -1, -1):
        adj_h = adj_h + courant * curl_with(inv_eps[None] * adj_e, diff_fwd)
        grad = grad + courant * jnp.sum(adj_e * curls[step], axis=0)
        adj_e = adj_e - courant * curl_with(adj_h, diff_bwd)
    voxel_grad = jax.ops.segment_sum(grad.reshape(-1), voxel_ids.reshape(-1).astype(jnp.int32), num_segments=VOX)
    return e_field, h_field, voxel_grad
```

```python
import jax
import jax.numpy as jnp
from jax import lax
from jax.experimental import pallas as pl
from jax.experimental.pallas import tpu as pltpu
from jax.sharding import PartitionSpec as P

STEPS = 4
COURANT = 0.5
MESH = pl.DeviceIdType.MESH
VOX_DEV = 64
UNROLL = 1


def make_kernel(ng, nb, nx, nz, ny):
    n = ng * nb
    steps = STEPS
    lo_row, hi_row = 8, 8 + nz

    def kernel(e_in, h_in, eps_in, ce_in, ch_in, ids_in, e_out, h_out, v_out,
               E, H, G, AH, AE, CURL, eps, ids, h0, ah0, zs, zl, S, R, part,
               in_sem, out_sem, xs_sem, xr_sem, zs_sem, zr_sem, as_sem, ar_sem):
        grp = lax.axis_index("grp")
        blk = lax.axis_index("blk")
        me = grp * nb + blk
        lane = lax.broadcasted_iota(jnp.int32, (nz, ny), 1)

        loads = [
            pltpu.make_async_copy(ce_in, AE.at[0], in_sem.at[0]),
            pltpu.make_async_copy(eps_in, eps, in_sem.at[1]),
            pltpu.make_async_copy(e_in, E.at[0, :, 0:nx, 0:nz, :], in_sem.at[2]),
            pltpu.make_async_copy(h_in, h0, in_sem.at[3]),
            pltpu.make_async_copy(ch_in, ah0, in_sem.at[4]),
            pltpu.make_async_copy(ids_in, ids, in_sem.at[5]),
        ]
        for load in loads:
            load.start()

        barrier = pltpu.get_barrier_semaphore()

        @pl.loop(1, n)
        def _(j):
            other = (me + j) % n
            pl.semaphore_signal(barrier, inc=1, device_id=(other // nb, other % nb), device_id_type=MESH)

        @pl.when(blk == nb - 1)
        def _():
            E[0:steps, 1:3, nx, 0:nz, :] = jnp.zeros((steps, 2, nz, ny), jnp.float32)
            G[:, 1:3, nx, 0:nz, :] = jnp.zeros((steps - 1, 2, nz, ny), jnp.float32)

        @pl.when(blk == 0)
        def _():
            H[:, 1:3, 0, lo_row:hi_row, :] = jnp.zeros((steps, 2, nz, ny), jnp.float32)
            AH[:, 1:3, 0, lo_row:hi_row, :] = jnp.zeros((steps - 1, 2, nz, ny), jnp.float32)

        rounds = 4 * steps - 2
        for r in range(rounds):
            edge = ng - 1 if r % 2 == 0 else 0

            @pl.when(grp == edge)
            def _(r=r):
                zl[r] = jnp.zeros((2, nx, ny), jnp.float32)

        def xcopy(r, buf):
            if r % 2 == 0:
                src, dst, to = buf.at[1:3, 0, 0:nz, :], buf.at[1:3, nx, 0:nz, :], blk - 1
            else:
                src, dst, to = buf.at[1:3, nx, lo_row:hi_row, :], buf.at[1:3, 0, lo_row:hi_row, :], blk + 1
            return pltpu.make_async_remote_copy(src, dst, xs_sem.at[r], xr_sem.at[r], device_id=(grp, to), device_id_type=MESH)

        def zcopy(r):
            to = grp - 1 if r % 2 == 0 else grp + 1
            return pltpu.make_async_remote_copy(zs.at[r], zl.at[r], zs_sem.at[r], zr_sem.at[r], device_id=(to, blk), device_id_type=MESH)

        def x_sends(r):
            return blk > 0 if r % 2 == 0 else blk < nb - 1

        def x_gets(r):
            return blk < nb - 1 if r % 2 == 0 else blk > 0

        def z_sends(r):
            return grp > 0 if r % 2 == 0 else grp < ng - 1

        def z_gets(r):
            return grp < ng - 1 if r % 2 == 0 else grp > 0

        used = []

        def send(r, buf):
            used.append((r, buf))

            @pl.when(x_sends(r))
            def _():
                xcopy(r, buf).start()

            @pl.when(z_sends(r))
            def _():
                zcopy(r).start()

        def get_z(r, buf):
            @pl.when(z_gets(r))
            def _():
                zcopy(r).wait_recv()

            for c in range(2):
                for i in range(nx):
                    if r % 2 == 0:
                        buf[c, i, nz:nz + 1, :] = zl[r, c, i:i + 1, :]
                    else:
                        buf[c, i + 1, lo_row - 1:lo_row, :] = zl[r, c, i:i + 1, :]

        def get_x(r, buf):
            @pl.when(x_gets(r))
            def _():
                xcopy(r, buf).wait_recv()

        def curl_f(buf, i):
            vx, vy, vz = (buf[c, i, 0:nz, :] for c in range(3))

            def dy(v):
                return jnp.where(lane == ny - 1, 0.0, pltpu.roll(v, ny - 1, 1)) - v

            dxy, dxz = (buf[c, i + 1, 0:nz, :] - v for c, v in ((1, vy), (2, vz)))
            dzx, dzy = (buf[c, i, 1:nz + 1, :] - v for c, v in ((0, vx), (1, vy)))
            return dy(vz) - dzy, dzx - dxz, dxy - dy(vx)

        def curl_b(buf, i):
            vx, vy, vz = (buf[c, i + 1, lo_row:hi_row, :] for c in range(3))

            def dy(v):
                return v - jnp.where(lane == 0, 0.0, pltpu.roll(v, 1, 1))

            dxy, dxz = (v - buf[c, i, lo_row:hi_row, :] for c, v in ((1, vy), (2, vz)))
            dzx, dzy = (v - buf[c, i + 1, lo_row - 1:hi_row - 1, :] for c, v in ((0, vx), (1, vy)))
            return dy(vz) - dzy, dzx - dxz, dxy - dy(vx)

        def each(first, last, body):
            def step(i, carry):
                body(i)
                return carry
            lax.fori_loop(first, last, step, 0, unroll=UNROLL)

        def f_step(r_in, src, prev, dst, r_out, sign):
            def body(i):
                cv = curl_f(src, i)
                for c in range(3):
                    new = prev(c, i) + sign * cv[c]
                    dst[c, i + 1, lo_row:hi_row, :] = new
                    if c < 2:
                        zs[r_out, c, pl.ds(i, 1), :] = new[nz - 1:nz, :]

            get_z(r_in, src)
            each(0, nx - 1, body)
            get_x(r_in, src)
            body(nx - 1)
            send(r_out, dst)

        def b_step(r_in, src, body):
            get_z(r_in, src)
            each(1, nx, body)
            get_x(r_in, src)
            body(0)

        loads[0].wait()
        loads[1].wait()

        def first_g(i):
            for c in range(3):
                g = eps[i] * AE[0, c, i]
                G[0, c, i, 0:nz, :] = g
                if c < 2:
                    zs[2 * steps, c, pl.ds(i, 1), :] = g[0:1, :]

        each(0, nx, first_g)
        loads[2].wait()
        for c in range(2):
            for i in range(nx):
                zs[0, c, i:i + 1, :] = E[0, c, i, 0:1, :]
        pl.semaphore_wait(barrier, n - 1)
        send(0, E.at[0])
        send(2 * steps, G.at[0])
        for load in loads[3:]:
            load.wait()

        for k in range(steps):
            rf, ra = 2 * k, 2 * steps + 2 * k
            adj = k < steps - 1
            if k == 0:
                h_prev = lambda c, i: h0[c, i]
                a_prev = lambda c, i: ah0[c, i]
            else:
                h_prev = lambda c, i, k=k: H[k - 1, c, i + 1, lo_row:hi_row, :]
                a_prev = lambda c, i, k=k: AH[k - 1, c, i + 1, lo_row:hi_row, :]
            f_step(rf, E.at[k], h_prev, H.at[k], rf + 1, -COURANT)
            if not adj:
                h_copy = pltpu.make_async_copy(H.at[k, :, 1:nx + 1, lo_row:hi_row, :], h_out, out_sem.at[0])
                h_copy.start()
            if adj:
                f_step(ra, G.at[k], a_prev, AH.at[k], ra + 1, COURANT)

            def e_body(i, k=k, rf=rf):
                cv = curl_b(H.at[k], i)
                scale = COURANT * eps[i]
                for c in range(3):
                    CURL[k, c, i] = cv[c]
                    new = E[k, c, i, 0:nz, :] + scale * cv[c]
                    E[k + 1, c, i, 0:nz, :] = new
                    if c < 2 and k < steps - 1:
                        zs[rf + 2, c, pl.ds(i, 1), :] = new[0:1, :]

            b_step(rf + 1, H.at[k], e_body)
            if k < steps - 1:
                send(rf + 2, E.at[k + 1])
            else:
                e_copy = pltpu.make_async_copy(E.at[steps, :, 0:nx, 0:nz, :], e_out, out_sem.at[1])
                e_copy.start()
            if adj:
                def a_body(i, k=k, ra=ra):
                    cv = curl_b(AH.at[k], i)
                    scale = eps[i]
                    for c in range(3):
                        new = AE[k, c, i] - COURANT * cv[c]
                        AE[k + 1, c, i] = new
                        if k < steps - 2:
                            g = scale * new
                            G[k + 1, c, i, 0:nz, :] = g
                            if c < 2:
                                zs[ra + 2, c, pl.ds(i, 1), :] = g[0:1, :]

                b_step(ra + 1, AH.at[k], a_body)
                if k < steps - 2:
                    send(ra + 2, G.at[k + 1])

        own = lax.broadcasted_iota(jnp.int32, (n, ny), 0)
        place = lax.broadcasted_iota(jnp.int32, (VOX_DEV, ny), 0)
        part[...] = jnp.zeros_like(part)

        def seg(i):
            grad = jnp.zeros((nz, ny), jnp.float32)
            for k in range(steps):
                for c in range(3):
                    grad = grad + AE[steps - 1 - k, c, i] * CURL[k, c, i]
            grad = COURANT * grad
            coarse = grad.astype(jnp.bfloat16).astype(jnp.float32)
            fine = grad - coarse
            v = ids[i]
            high, low = v // VOX_DEV, v % VOX_DEV
            lhs, rhs = [], []
            for z in range(nz):
                hit = high[z:z + 1, :] == own
                lhs.append(jnp.concatenate([
                    jnp.where(hit, coarse[z:z + 1, :], 0.0).astype(jnp.bfloat16),
                    jnp.where(hit, fine[z:z + 1, :], 0.0).astype(jnp.bfloat16)], axis=0))
                rhs.append(jnp.where(low[z:z + 1, :] == place, 1.0, 0.0).astype(jnp.bfloat16))
            part[...] += lax.dot_general(
                jnp.concatenate(lhs, axis=1), jnp.concatenate(rhs, axis=1),
                (((1,), (1,)), ((), ())), preferred_element_type=jnp.float32)

        @pl.loop(0, nx)
        def _(i):
            seg(i)

        both = part[0:n, :] + part[n:2 * n, :]
        both = jnp.concatenate([both, jnp.zeros((n, 128 - VOX_DEV), jnp.float32)], axis=1)
        for d in range(n):
            S[d] = both[d:d + 1, :]

        @pl.loop(1, n)
        def _(j):
            to = (me + j) % n
            pltpu.make_async_remote_copy(
                S.at[to], R.at[me], as_sem, ar_sem,
                device_id=(to // nb, to % nb), device_id_type=MESH).start()

        R[me] = S[me]
        rest = pl.ds(0, n - 1)
        pltpu.make_async_copy(R.at[rest], R.at[rest], ar_sem).wait()
        v_out[...] = jnp.sum(R[...], axis=0)[:, 0:VOX_DEV]
        pltpu.make_async_copy(S.at[rest], S.at[rest], as_sem).wait()
        h_copy.wait()
        e_copy.wait()
        for r, buf in used:
            @pl.when(x_sends(r))
            def _(r=r, buf=buf):
                xcopy(r, buf).wait_send()

            @pl.when(z_sends(r))
            def _(r=r):
                zcopy(r).wait_send()

    return kernel


def solution(mesh):
    ng, nb = mesh.shape["grp"], mesh.shape["blk"]
    n = ng * nb

    def local(e_field, h_field, inv_eps, cot_e, cot_h, voxel_ids):
        _, nx, nz, ny = e_field.shape
        f32 = jnp.float32
        padded = (3, nx + 1, nz + 8, ny)
        plain = (3, nx, nz, ny)
        rounds = 4 * STEPS - 2
        dma = pltpu.SemaphoreType.DMA
        hbm = pl.BlockSpec(memory_space=pl.ANY)
        e_new, h_new, vox = pl.pallas_call(
            make_kernel(ng, nb, nx, nz, ny),
            out_shape=(
                jax.ShapeDtypeStruct(plain, f32),
                jax.ShapeDtypeStruct(plain, f32),
                jax.ShapeDtypeStruct((1, VOX_DEV), f32),
            ),
            in_specs=[hbm] * 6,
            out_specs=(hbm, hbm, pl.BlockSpec(memory_space=pltpu.VMEM)),
            scratch_shapes=[
                pltpu.VMEM((STEPS + 1,) + padded, f32),
                pltpu.VMEM((STEPS,) + padded, f32),
                pltpu.VMEM((STEPS - 1,) + padded, f32),
                pltpu.VMEM((STEPS - 1,) + padded, f32),
                pltpu.VMEM((STEPS,) + plain, f32),
                pltpu.VMEM((STEPS,) + plain, f32),
                pltpu.VMEM(plain[1:], f32),
                pltpu.VMEM(plain[1:], jnp.int32),
                pltpu.VMEM(plain, f32),
                pltpu.VMEM(plain, f32),
                pltpu.VMEM((rounds, 2, nx, ny), f32),
                pltpu.VMEM((rounds, 2, nx, ny), f32),
                pltpu.VMEM((n, 1, 128), f32),
                pltpu.VMEM((n, 1, 128), f32),
                pltpu.VMEM((2 * n, VOX_DEV), f32),
                dma((6,)), dma((2,)), dma((rounds,)), dma((rounds,)),
                dma((rounds,)), dma((rounds,)), dma, dma,
            ],
            compiler_params=pltpu.CompilerParams(
                collective_id=0, has_side_effects=True, vmem_limit_bytes=40 * 1024 * 1024),
        )(e_field, h_field, inv_eps, cot_e, cot_h, voxel_ids)
        return e_new, h_new, vox.reshape(VOX_DEV)

    field, cell = P(None, "blk", "grp", None), P("blk", "grp", None)
    return jax.shard_map(
        local, mesh=mesh,
        in_specs=(field, field, cell, field, field, cell),
        out_specs=(field, field, P(("grp", "blk"))),
        check_vma=False,
    )
```

```python
import jax
import jax.numpy as jnp
from jax import lax
from jax.experimental import pallas as pl
from jax.experimental.pallas import tpu as pltpu
from jax.sharding import PartitionSpec as P

STEPS = 4
COURANT = 0.5
MESH = pl.DeviceIdType.MESH
VOX_DEV = 64
UNROLL = True


def make_kernel(ng, nb, nx, nz, ny):
    n = ng * nb
    steps = STEPS
    lo_row, hi_row = 8, 8 + nz

    def kernel(e_in, h_in, eps_in, ce_in, ch_in, ids_in, e_out, h_out, v_out,
               E, H, G, AH, AE, CURL, eps, ids, h0, ah0, zs, zl, S, R, part,
               in_sem, out_sem, xs_sem, xr_sem, zs_sem, zr_sem, as_sem, ar_sem):
        grp = lax.axis_index("grp")
        blk = lax.axis_index("blk")
        me = grp * nb + blk
        lane = lax.broadcasted_iota(jnp.int32, (nz, ny), 1)

        loads = [
            pltpu.make_async_copy(ce_in, AE.at[0], in_sem.at[0]),
            pltpu.make_async_copy(eps_in, eps, in_sem.at[1]),
            pltpu.make_async_copy(e_in, E.at[0, :, 0:nx, 0:nz, :], in_sem.at[2]),
            pltpu.make_async_copy(h_in, h0, in_sem.at[3]),
            pltpu.make_async_copy(ch_in, ah0, in_sem.at[4]),
            pltpu.make_async_copy(ids_in, ids, in_sem.at[5]),
        ]
        for load in loads:
            load.start()

        barrier = pltpu.get_barrier_semaphore()

        @pl.loop(1, n)
        def _(j):
            other = (me + j) % n
            pl.semaphore_signal(barrier, inc=1, device_id=(other // nb, other % nb), device_id_type=MESH)

        @pl.when(blk == nb - 1)
        def _():
            E[0:steps, 1:3, nx, 0:nz, :] = jnp.zeros((steps, 2, nz, ny), jnp.float32)
            G[:, 1:3, nx, 0:nz, :] = jnp.zeros((steps - 1, 2, nz, ny), jnp.float32)

        @pl.when(blk == 0)
        def _():
            H[:, 1:3, 0, lo_row:hi_row, :] = jnp.zeros((steps, 2, nz, ny), jnp.float32)
            AH[:, 1:3, 0, lo_row:hi_row, :] = jnp.zeros((steps - 1, 2, nz, ny), jnp.float32)

        rounds = 4 * steps - 2
        for r in range(rounds):
            edge = ng - 1 if r % 2 == 0 else 0

            @pl.when(grp == edge)
            def _(r=r):
                zl[r] = jnp.zeros((2, nx, ny), jnp.float32)

        def xcopy(r, buf):
            if r % 2 == 0:
                src, dst, to = buf.at[1:3, 0, 0:nz, :], buf.at[1:3, nx, 0:nz, :], blk - 1
            else:
                src, dst, to = buf.at[1:3, nx, lo_row:hi_row, :], buf.at[1:3, 0, lo_row:hi_row, :], blk + 1
            return pltpu.make_async_remote_copy(src, dst, xs_sem.at[r], xr_sem.at[r], device_id=(grp, to), device_id_type=MESH)

        def zcopy(r):
            to = grp - 1 if r % 2 == 0 else grp + 1
            return pltpu.make_async_remote_copy(zs.at[r], zl.at[r], zs_sem.at[r], zr_sem.at[r], device_id=(to, blk), device_id_type=MESH)

        def x_sends(r):
            return blk > 0 if r % 2 == 0 else blk < nb - 1

        def x_gets(r):
            return blk < nb - 1 if r % 2 == 0 else blk > 0

        def z_sends(r):
            return grp > 0 if r % 2 == 0 else grp < ng - 1

        def z_gets(r):
            return grp < ng - 1 if r % 2 == 0 else grp > 0

        used = []

        def send(r, buf):
            used.append((r, buf))

            @pl.when(x_sends(r))
            def _():
                xcopy(r, buf).start()

            @pl.when(z_sends(r))
            def _():
                zcopy(r).start()

        def get_z(r, buf):
            @pl.when(z_gets(r))
            def _():
                zcopy(r).wait_recv()

            for c in range(2):
                for i in range(nx):
                    if r % 2 == 0:
                        buf[c, i, nz:nz + 1, :] = zl[r, c, i:i + 1, :]
                    else:
                        buf[c, i + 1, lo_row - 1:lo_row, :] = zl[r, c, i:i + 1, :]

        def get_x(r, buf):
            @pl.when(x_gets(r))
            def _():
                xcopy(r, buf).wait_recv()

        def curl_f(buf, i):
            vx, vy, vz = (buf[c, i, 0:nz, :] for c in range(3))

            def dy(v):
                return jnp.where(lane == ny - 1, 0.0, pltpu.roll(v, ny - 1, 1)) - v

            dxy, dxz = (buf[c, i + 1, 0:nz, :] - v for c, v in ((1, vy), (2, vz)))
            dzx, dzy = (buf[c, i, 1:nz + 1, :] - v for c, v in ((0, vx), (1, vy)))
            return dy(vz) - dzy, dzx - dxz, dxy - dy(vx)

        def curl_b(buf, i):
            vx, vy, vz = (buf[c, i + 1, lo_row:hi_row, :] for c in range(3))

            def dy(v):
                return v - jnp.where(lane == 0, 0.0, pltpu.roll(v, 1, 1))

            dxy, dxz = (v - buf[c, i, lo_row:hi_row, :] for c, v in ((1, vy), (2, vz)))
            dzx, dzy = (v - buf[c, i + 1, lo_row - 1:hi_row - 1, :] for c, v in ((0, vx), (1, vy)))
            return dy(vz) - dzy, dzx - dxz, dxy - dy(vx)

        def each(first, last, body):
            def step(i, carry):
                body(i)
                return carry
            lax.fori_loop(first, last, step, 0, unroll=UNROLL)

        def f_step(r_in, src, prev, dst, r_out, sign):
            def body(i):
                cv = curl_f(src, i)
                for c in range(3):
                    new = prev(c, i) + sign * cv[c]
                    dst[c, i + 1, lo_row:hi_row, :] = new
                    if c < 2:
                        zs[r_out, c, pl.ds(i, 1), :] = new[nz - 1:nz, :]

            get_z(r_in, src)
            each(0, nx - 1, body)
            get_x(r_in, src)
            body(nx - 1)
            send(r_out, dst)

        def b_step(r_in, src, body):
            get_z(r_in, src)
            each(1, nx, body)
            get_x(r_in, src)
            body(0)

        loads[0].wait()
        loads[1].wait()

        def first_g(i):
            for c in range(3):
                g = eps[i] * AE[0, c, i]
                G[0, c, i, 0:nz, :] = g
                if c < 2:
                    zs[2 * steps, c, pl.ds(i, 1), :] = g[0:1, :]

        each(0, nx, first_g)
        loads[2].wait()
        for c in range(2):
            for i in range(nx):
                zs[0, c, i:i + 1, :] = E[0, c, i, 0:1, :]
        pl.semaphore_wait(barrier, n - 1)
        send(0, E.at[0])
        send(2 * steps, G.at[0])
        for load in loads[3:]:
            load.wait()

        for k in range(steps):
            rf, ra = 2 * k, 2 * steps + 2 * k
            adj = k < steps - 1
            if k == 0:
                h_prev = lambda c, i: h0[c, i]
                a_prev = lambda c, i: ah0[c, i]
            else:
                h_prev = lambda c, i, k=k: H[k - 1, c, i + 1, lo_row:hi_row, :]
                a_prev = lambda c, i, k=k: AH[k - 1, c, i + 1, lo_row:hi_row, :]
            f_step(rf, E.at[k], h_prev, H.at[k], rf + 1, -COURANT)
            if not adj:
                h_copy = pltpu.make_async_copy(H.at[k, :, 1:nx + 1, lo_row:hi_row, :], h_out, out_sem.at[0])
                h_copy.start()
            if adj:
                f_step(ra, G.at[k], a_prev, AH.at[k], ra + 1, COURANT)

            def e_body(i, k=k, rf=rf):
                cv = curl_b(H.at[k], i)
                scale = COURANT * eps[i]
                for c in range(3):
                    CURL[k, c, i] = cv[c]
                    new = E[k, c, i, 0:nz, :] + scale * cv[c]
                    E[k + 1, c, i, 0:nz, :] = new
                    if c < 2 and k < steps - 1:
                        zs[rf + 2, c, pl.ds(i, 1), :] = new[0:1, :]

            b_step(rf + 1, H.at[k], e_body)
            if k < steps - 1:
                send(rf + 2, E.at[k + 1])
            else:
                e_copy = pltpu.make_async_copy(E.at[steps, :, 0:nx, 0:nz, :], e_out, out_sem.at[1])
                e_copy.start()
            if adj:
                def a_body(i, k=k, ra=ra):
                    cv = curl_b(AH.at[k], i)
                    scale = eps[i]
                    for c in range(3):
                        new = AE[k, c, i] - COURANT * cv[c]
                        AE[k + 1, c, i] = new
                        if k < steps - 2:
                            g = scale * new
                            G[k + 1, c, i, 0:nz, :] = g
                            if c < 2:
                                zs[ra + 2, c, pl.ds(i, 1), :] = g[0:1, :]

                b_step(ra + 1, AH.at[k], a_body)
                if k < steps - 2:
                    send(ra + 2, G.at[k + 1])

        own = lax.broadcasted_iota(jnp.int32, (n, ny), 0)
        place = lax.broadcasted_iota(jnp.int32, (VOX_DEV, ny), 0)
        part[...] = jnp.zeros_like(part)

        def seg(i):
            grad = jnp.zeros((nz, ny), jnp.float32)
            for k in range(steps):
                for c in range(3):
                    grad = grad + AE[steps - 1 - k, c, i] * CURL[k, c, i]
            grad = COURANT * grad
            coarse = grad.astype(jnp.bfloat16).astype(jnp.float32)
            fine = grad - coarse
            v = ids[i]
            high, low = v // VOX_DEV, v % VOX_DEV
            lhs, rhs = [], []
            for z in range(nz):
                hit = high[z:z + 1, :] == own
                lhs.append(jnp.concatenate([
                    jnp.where(hit, coarse[z:z + 1, :], 0.0).astype(jnp.bfloat16),
                    jnp.where(hit, fine[z:z + 1, :], 0.0).astype(jnp.bfloat16)], axis=0))
                rhs.append(jnp.where(low[z:z + 1, :] == place, 1.0, 0.0).astype(jnp.bfloat16))
            part[...] += lax.dot_general(
                jnp.concatenate(lhs, axis=1), jnp.concatenate(rhs, axis=1),
                (((1,), (1,)), ((), ())), preferred_element_type=jnp.float32)

        @pl.loop(0, nx)
        def _(i):
            seg(i)

        both = part[0:n, :] + part[n:2 * n, :]
        both = jnp.concatenate([both, jnp.zeros((n, 128 - VOX_DEV), jnp.float32)], axis=1)
        for d in range(n):
            S[d] = both[d:d + 1, :]

        @pl.loop(1, n)
        def _(j):
            to = (me + j) % n
            pltpu.make_async_remote_copy(
                S.at[to], R.at[me], as_sem, ar_sem,
                device_id=(to // nb, to % nb), device_id_type=MESH).start()

        R[me] = S[me]
        rest = pl.ds(0, n - 1)
        pltpu.make_async_copy(R.at[rest], R.at[rest], ar_sem).wait()
        v_out[...] = jnp.sum(R[...], axis=0)[:, 0:VOX_DEV]
        pltpu.make_async_copy(S.at[rest], S.at[rest], as_sem).wait()
        h_copy.wait()
        e_copy.wait()
        for r, buf in used:
            @pl.when(x_sends(r))
            def _(r=r, buf=buf):
                xcopy(r, buf).wait_send()

            @pl.when(z_sends(r))
            def _(r=r):
                zcopy(r).wait_send()

    return kernel


def solution(mesh):
    ng, nb = mesh.shape["grp"], mesh.shape["blk"]
    n = ng * nb

    def local(e_field, h_field, inv_eps, cot_e, cot_h, voxel_ids):
        _, nx, nz, ny = e_field.shape
        f32 = jnp.float32
        padded = (3, nx + 1, nz + 8, ny)
        plain = (3, nx, nz, ny)
        rounds = 4 * STEPS - 2
        dma = pltpu.SemaphoreType.DMA
        hbm = pl.BlockSpec(memory_space=pl.ANY)
        e_new, h_new, vox = pl.pallas_call(
            make_kernel(ng, nb, nx, nz, ny),
            out_shape=(
                jax.ShapeDtypeStruct(plain, f32),
                jax.ShapeDtypeStruct(plain, f32),
                jax.ShapeDtypeStruct((1, VOX_DEV), f32),
            ),
            in_specs=[hbm] * 6,
            out_specs=(hbm, hbm, pl.BlockSpec(memory_space=pltpu.VMEM)),
            scratch_shapes=[
                pltpu.VMEM((STEPS + 1,) + padded, f32),
                pltpu.VMEM((STEPS,) + padded, f32),
                pltpu.VMEM((STEPS - 1,) + padded, f32),
                pltpu.VMEM((STEPS - 1,) + padded, f32),
                pltpu.VMEM((STEPS,) + plain, f32),
                pltpu.VMEM((STEPS,) + plain, f32),
                pltpu.VMEM(plain[1:], f32),
                pltpu.VMEM(plain[1:], jnp.int32),
                pltpu.VMEM(plain, f32),
                pltpu.VMEM(plain, f32),
                pltpu.VMEM((rounds, 2, nx, ny), f32),
                pltpu.VMEM((rounds, 2, nx, ny), f32),
                pltpu.VMEM((n, 1, 128), f32),
                pltpu.VMEM((n, 1, 128), f32),
                pltpu.VMEM((2 * n, VOX_DEV), f32),
                dma((6,)), dma((2,)), dma((rounds,)), dma((rounds,)),
                dma((rounds,)), dma((rounds,)), dma, dma,
            ],
            compiler_params=pltpu.CompilerParams(
                collective_id=0, has_side_effects=True, vmem_limit_bytes=60 * 1024 * 1024),
        )(e_field, h_field, inv_eps, cot_e, cot_h, voxel_ids)
        return e_new, h_new, vox.reshape(VOX_DEV)

    field, cell = P(None, "blk", "grp", None), P("blk", "grp", None)
    return jax.shard_map(
        local, mesh=mesh,
        in_specs=(field, field, cell, field, field, cell),
        out_specs=(field, field, P(("grp", "blk"))),
        check_vma=False,
    )
```

```python
import jax
import jax.numpy as jnp
from jax import lax
from jax.experimental import pallas as pl
from jax.experimental.pallas import tpu as pltpu
from jax.sharding import PartitionSpec as P

STEPS = 4
COURANT = 0.5
MESH = pl.DeviceIdType.MESH
VOX_DEV = 64
UNROLL = True


def make_kernel(ng, nb, nx, nz, ny):
    n = ng * nb
    steps = STEPS
    top, end = 8, 8 + nz

    def kernel(e_in, h_in, eps_in, ce_in, ch_in, ids_in, e_out, h_out, v_out,
               E, H, G, AH, AE, CURL, eps, ids, zs_dn, zl_dn, zs_up, zl_up, cl_a, cl_b, zs_h, zl_h,
               S, R, part, in_sem, out_sem, as_sem, ar_sem, *link_sems):
        xd, xu, zd, zu, ca, cb, hx, hz = (link_sems[2 * j:2 * j + 2] for j in range(8))
        grp = lax.axis_index("grp")
        blk = lax.axis_index("blk")
        me = grp * nb + blk
        lane = lax.broadcasted_iota(jnp.int32, (nz, ny), 1)
        lane_h = lax.broadcasted_iota(jnp.int32, (end, ny), 1)

        loads = [
            pltpu.make_async_copy(ce_in, AE.at[0], in_sem.at[0]),
            pltpu.make_async_copy(eps_in, eps, in_sem.at[1]),
            pltpu.make_async_copy(e_in, E.at[0, :, 1:nx + 1, top:end, :], in_sem.at[2]),
            pltpu.make_async_copy(h_in, H.at[0, :, 1:nx + 1, top:end, :], in_sem.at[3]),
            pltpu.make_async_copy(ch_in, AH.at[0, :, 1:nx + 1, top:end, :], in_sem.at[4]),
            pltpu.make_async_copy(ids_in, ids, in_sem.at[5]),
        ]
        for load in loads:
            load.start()

        barrier = pltpu.get_barrier_semaphore()

        @pl.loop(1, n)
        def _(j):
            other = (me + j) % n
            pl.semaphore_signal(barrier, inc=1, device_id=(other // nb, other % nb), device_id_type=MESH)

        first_x, last_x = blk == 0, blk == nb - 1
        first_z, last_z = grp == 0, grp == ng - 1
        rounds = 2 * steps - 1

        @pl.when(last_x)
        def _():
            E[0:steps, 1:3, nx + 1, top:end, :] = jnp.zeros((steps, 2, nz, ny), jnp.float32)
            G[:, 1:3, nx + 1, top:end, :] = jnp.zeros((steps - 1, 2, nz, ny), jnp.float32)

        @pl.when(first_x)
        def _():
            H[:, 1:3, 0, top:end, :] = jnp.zeros((steps + 1, 2, nz, ny), jnp.float32)
            AH[:, 1:3, 0, top:end, :] = jnp.zeros((steps, 2, nz, ny), jnp.float32)

        @pl.when(last_z)
        def _():
            zl_dn[...] = jnp.zeros_like(zl_dn)

        @pl.when(jnp.logical_or(last_z, first_x))
        def _():
            cl_a[...] = jnp.zeros_like(cl_a)

        @pl.when(jnp.logical_or(first_z, last_x))
        def _():
            cl_b[...] = jnp.zeros_like(cl_b)

        def remote(src, dst, sems, r, to):
            return pltpu.make_async_remote_copy(src, dst, sems[0].at[r], sems[1].at[r], device_id=to, device_id_type=MESH)

        def links(r, buf):
            yes_dn, yes_up = jnp.logical_not(first_x), jnp.logical_not(last_x)
            z_dn, z_up = jnp.logical_not(first_z), jnp.logical_not(last_z)
            both = jnp.logical_and
            return [
                (yes_dn, yes_up, remote(buf.at[1:3, 1, top:end, :], buf.at[1:3, nx + 1, top:end, :], xd, r, (grp, blk - 1))),
                (yes_up, yes_dn, remote(buf.at[:, nx, top:end, :], buf.at[:, 0, top:end, :], xu, r, (grp, blk + 1))),
                (z_dn, z_up, remote(zs_dn.at[r], zl_dn.at[r], zd, r, (grp - 1, blk))),
                (z_up, z_dn, remote(zs_up.at[r], zl_up.at[r], zu, r, (grp + 1, blk))),
                (both(z_dn, yes_up), both(z_up, yes_dn), remote(zs_dn.at[r, 0, nx - 1], cl_a.at[r], ca, r, (grp - 1, blk + 1))),
                (both(z_up, yes_dn), both(z_dn, yes_up), remote(zs_up.at[r, 2, 0], cl_b.at[r], cb, r, (grp + 1, blk - 1))),
            ]

        def start_links(r, buf, h0=None):
            jobs = [links(r, buf), hlinks(r, h0) if h0 is not None else []]
            for sends, _, copy in jobs[0] + jobs[1]:
                used.append((sends, copy))
                pl.when(sends)(copy.start)

        def hlinks(r, h0):
            q = 0 if r == 0 else 1
            return [
                (jnp.logical_not(last_x), jnp.logical_not(first_x), remote(h0.at[1:3, nx, top:end, :], h0.at[1:3, 0, top:end, :], hx, q, (grp, blk + 1))),
                (jnp.logical_not(last_z), jnp.logical_not(first_z), remote(zs_h.at[q], zl_h.at[q], hz, q, (grp + 1, blk))),
            ]

        used = []

        def finish_links(r, buf, h0=None):
            jobs = links(r, buf) + (hlinks(r, h0) if h0 is not None else [])
            for _, gets, copy in jobs:
                pl.when(gets)(copy.wait_recv)
            for c in range(2):
                for i in range(nx):
                    buf[c, i + 1, end:end + 1, :] = zl_dn[r, c, i]
            buf[0, 0, end:end + 1, :] = cl_a[r]
            buf[2, nx + 1, top - 1:top, :] = cl_b[r]

            @pl.when(jnp.logical_not(first_z))
            def _():
                for c in range(3):
                    for i in range(nx):
                        buf[c, i + 1, top - 1:top, :] = zl_up[r, c, i]
                if h0 is not None:
                    for c in range(2):
                        for i in range(nx):
                            h0[c, i + 1, top - 1:top, :] = zl_h[0 if r == 0 else 1, c, i]

        def curl_f(buf, i):
            vx, vy, vz = (buf[c, i, 0:end, :] for c in range(3))

            def dy(v):
                return jnp.where(lane_h == ny - 1, 0.0, pltpu.roll(v, ny - 1, 1)) - v

            dxy, dxz = (buf[c, i + 1, 0:end, :] - v for c, v in ((1, vy), (2, vz)))
            dzx, dzy = (buf[c, i, 1:end + 1, :] - v for c, v in ((0, vx), (1, vy)))
            return dy(vz) - dzy, dzx - dxz, dxy - dy(vx)

        def curl_b(buf, i):
            vx, vy, vz = (buf[c, i, top:end, :] for c in range(3))

            def dy(v):
                return v - jnp.where(lane == 0, 0.0, pltpu.roll(v, 1, 1))

            dxy, dxz = (v - buf[c, i - 1, top:end, :] for c, v in ((1, vy), (2, vz)))
            dzx, dzy = (v - buf[c, i, top - 1:end - 1, :] for c, v in ((0, vx), (1, vy)))
            return dy(vz) - dzy, dzx - dxz, dxy - dy(vx)

        def each(first, last, body):
            def step(i, carry):
                body(i)
                return carry
            lax.fori_loop(first, last, step, 0, unroll=UNROLL)

        def f_step(src, prev, dst, sign):
            def body(i):
                cv = curl_f(src, i)
                for c in range(3):
                    dst[c, i, 0:end, :] = prev[c, i, 0:end, :] + sign * cv[c]

            @pl.when(jnp.logical_not(first_x))
            def _():
                vx, vy, vz = (src[c, 0, top:end, :] for c in range(3))

                def dy(v):
                    return jnp.where(lane == ny - 1, 0.0, pltpu.roll(v, ny - 1, 1)) - v

                cy = (src[0, 0, top + 1:end + 1, :] - vx) - (src[2, 1, top:end, :] - vz)
                cz = (src[1, 1, top:end, :] - vy) - dy(vx)
                dst[1, 0, top:end, :] = prev[1, 0, top:end, :] + sign * cy
                dst[2, 0, top:end, :] = prev[2, 0, top:end, :] + sign * cz

            each(1, nx + 1, body)

            @pl.when(first_z)
            def _():
                for c in range(2):
                    for i in range(1, nx + 1):
                        dst[c, i, top - 1:top, :] = jnp.zeros((1, ny), jnp.float32)

        def edge_rows(r, c, i, new):
            if c < 2:
                zs_dn[r, c, i - 1] = new[0:1, :]
            zs_up[r, c, i - 1] = new[nz - 1:nz, :]

        ra = steps
        loads[0].wait()
        loads[1].wait()

        def first_g(i):
            for c in range(3):
                g = eps[i - 1] * AE[0, c, i - 1]
                G[0, c, i, top:end, :] = g
                edge_rows(ra, c, i, g)

        each(1, nx + 1, first_g)
        for load in loads[2:5]:
            load.wait()
        for i in range(1, nx + 1):
            for c in range(3):
                edge_rows(0, c, i, E[0, c, i, top:end, :])
            for c in range(2):
                zs_h[0, c, i - 1] = H[0, c, i, end - 1:end, :]
                zs_h[1, c, i - 1] = AH[0, c, i, end - 1:end, :]
        pl.semaphore_wait(barrier, n - 1)
        start_links(0, E.at[0], H.at[0])
        start_links(ra, G.at[0], AH.at[0])
        loads[5].wait()

        for k in range(steps):
            finish_links(k, E.at[k], H.at[0] if k == 0 else None)
            f_step(E.at[k], H.at[k], H.at[k + 1], -COURANT)
            if k == steps - 1:
                h_copy = pltpu.make_async_copy(H.at[steps, :, 1:nx + 1, top:end, :], h_out, out_sem.at[0])
                h_copy.start()

            def e_body(i, k=k):
                cv = curl_b(H.at[k + 1], i)
                scale = COURANT * eps[i - 1]
                for c in range(3):
                    CURL[k, c, i - 1] = cv[c]
                    new = E[k, c, i, top:end, :] + scale * cv[c]
                    E[k + 1, c, i, top:end, :] = new
                    if k < steps - 1:
                        edge_rows(k + 1, c, i, new)

            each(1, nx + 1, e_body)
            if k == steps - 1:
                e_copy = pltpu.make_async_copy(E.at[steps, :, 1:nx + 1, top:end, :], e_out, out_sem.at[1])
                e_copy.start()
                continue
            start_links(k + 1, E.at[k + 1])
            finish_links(ra + k, G.at[k], AH.at[0] if k == 0 else None)
            f_step(G.at[k], AH.at[k], AH.at[k + 1], COURANT)

            def a_body(i, k=k):
                cv = curl_b(AH.at[k + 1], i)
                for c in range(3):
                    new = AE[k, c, i - 1] - COURANT * cv[c]
                    AE[k + 1, c, i - 1] = new
                    if k < steps - 2:
                        g = eps[i - 1] * new
                        G[k + 1, c, i, top:end, :] = g
                        edge_rows(ra + k + 1, c, i, g)

            each(1, nx + 1, a_body)
            if k < steps - 2:
                start_links(ra + k + 1, G.at[k + 1])

        own = lax.broadcasted_iota(jnp.int32, (n, ny), 0)
        place = lax.broadcasted_iota(jnp.int32, (VOX_DEV, ny), 0)
        part[...] = jnp.zeros_like(part)

        def seg(i):
            grad = jnp.zeros((nz, ny), jnp.float32)
            for k in range(steps):
                for c in range(3):
                    grad = grad + AE[steps - 1 - k, c, i] * CURL[k, c, i]
            grad = COURANT * grad
            coarse = grad.astype(jnp.bfloat16).astype(jnp.float32)
            fine = grad - coarse
            v = ids[i]
            high, low = v // VOX_DEV, v % VOX_DEV
            lhs, rhs = [], []
            for z in range(nz):
                hit = high[z:z + 1, :] == own
                lhs.append(jnp.concatenate([
                    jnp.where(hit, coarse[z:z + 1, :], 0.0).astype(jnp.bfloat16),
                    jnp.where(hit, fine[z:z + 1, :], 0.0).astype(jnp.bfloat16)], axis=0))
                rhs.append(jnp.where(low[z:z + 1, :] == place, 1.0, 0.0).astype(jnp.bfloat16))
            part[...] += lax.dot_general(
                jnp.concatenate(lhs, axis=1), jnp.concatenate(rhs, axis=1),
                (((1,), (1,)), ((), ())), preferred_element_type=jnp.float32)

        @pl.loop(0, nx)
        def _(i):
            seg(i)

        both = part[0:n, :] + part[n:2 * n, :]
        both = jnp.concatenate([both, jnp.zeros((n, 128 - VOX_DEV), jnp.float32)], axis=1)
        for d in range(n):
            S[d] = both[d:d + 1, :]

        @pl.loop(1, n)
        def _(j):
            to = (me + j) % n
            pltpu.make_async_remote_copy(
                S.at[to], R.at[me], as_sem, ar_sem,
                device_id=(to // nb, to % nb), device_id_type=MESH).start()

        R[me] = S[me]
        rest = pl.ds(0, n - 1)
        pltpu.make_async_copy(R.at[rest], R.at[rest], ar_sem).wait()
        v_out[...] = jnp.sum(R[...], axis=0)[:, 0:VOX_DEV]
        pltpu.make_async_copy(S.at[rest], S.at[rest], as_sem).wait()
        h_copy.wait()
        e_copy.wait()
        for sends, copy in used:
            pl.when(sends)(copy.wait_send)

    return kernel


def solution(mesh):
    ng, nb = mesh.shape["grp"], mesh.shape["blk"]
    n = ng * nb

    def local(e_field, h_field, inv_eps, cot_e, cot_h, voxel_ids):
        _, nx, nz, ny = e_field.shape
        f32 = jnp.float32
        padded = (3, nx + 2, nz + 16, ny)
        plain = (3, nx, nz, ny)
        rounds = 2 * STEPS - 1
        dma = pltpu.SemaphoreType.DMA
        hbm = pl.BlockSpec(memory_space=pl.ANY)
        e_new, h_new, vox = pl.pallas_call(
            make_kernel(ng, nb, nx, nz, ny),
            out_shape=(
                jax.ShapeDtypeStruct(plain, f32),
                jax.ShapeDtypeStruct(plain, f32),
                jax.ShapeDtypeStruct((1, VOX_DEV), f32),
            ),
            in_specs=[hbm] * 6,
            out_specs=(hbm, hbm, pl.BlockSpec(memory_space=pltpu.VMEM)),
            scratch_shapes=[
                pltpu.VMEM((STEPS + 1,) + padded, f32),
                pltpu.VMEM((STEPS + 1,) + padded, f32),
                pltpu.VMEM((STEPS - 1,) + padded, f32),
                pltpu.VMEM((STEPS,) + padded, f32),
                pltpu.VMEM((STEPS,) + plain, f32),
                pltpu.VMEM((STEPS,) + plain, f32),
                pltpu.VMEM(plain[1:], f32),
                pltpu.VMEM(plain[1:], jnp.int32),
                pltpu.VMEM((rounds, 2, nx, 1, ny), f32),
                pltpu.VMEM((rounds, 2, nx, 1, ny), f32),
                pltpu.VMEM((rounds, 3, nx, 1, ny), f32),
                pltpu.VMEM((rounds, 3, nx, 1, ny), f32),
                pltpu.VMEM((rounds, 1, ny), f32),
                pltpu.VMEM((rounds, 1, ny), f32),
                pltpu.VMEM((2, 2, nx, 1, ny), f32),
                pltpu.VMEM((2, 2, nx, 1, ny), f32),
                pltpu.VMEM((n, 1, 128), f32),
                pltpu.VMEM((n, 1, 128), f32),
                pltpu.VMEM((2 * n, VOX_DEV), f32),
                dma((6,)), dma((2,)), dma, dma,
            ] + [dma((rounds,))] * 12 + [dma((2,))] * 4,
            compiler_params=pltpu.CompilerParams(
                collective_id=0, has_side_effects=True, vmem_limit_bytes=60 * 1024 * 1024),
        )(e_field, h_field, inv_eps, cot_e, cot_h, voxel_ids)
        return e_new, h_new, vox.reshape(VOX_DEV)

    field, cell = P(None, "blk", "grp", None), P("blk", "grp", None)
    return jax.shard_map(
        local, mesh=mesh,
        in_specs=(field, field, cell, field, field, cell),
        out_specs=(field, field, P(("grp", "blk"))),
        check_vma=False,
    )
```

```python
import jax
import jax.numpy as jnp
from jax import lax
from jax.experimental import pallas as pl
from jax.experimental.pallas import tpu as pltpu
from jax.sharding import PartitionSpec as P

STEPS = 4
COURANT = 0.5
MESH = pl.DeviceIdType.MESH
VOX_DEV = 64
UNROLL = True


def make_kernel(ng, nb, nx, nz, ny):
    n = ng * nb
    steps = STEPS
    top, end = 8, 8 + nz

    def kernel(e_in, h_in, eps_in, ce_in, ch_in, ids_in, e_out, h_out, v_out,
               E, H, G, AH, AE, CURL, eps, ids, zs_dn, zl_dn, zs_up, zl_up, cl_a, cl_b, zs_h, zl_h,
               S, R, part, in_sem, out_sem, as_sem, ar_sem, *link_sems):
        xd, xu, zd, zu, ca, cb, hx, hz = (link_sems[2 * j:2 * j + 2] for j in range(8))
        grp = lax.axis_index("grp")
        blk = lax.axis_index("blk")
        me = grp * nb + blk
        lane = lax.broadcasted_iota(jnp.int32, (nz, ny), 1)
        lane_h = lax.broadcasted_iota(jnp.int32, (end, ny), 1)

        loads = [
            pltpu.make_async_copy(ce_in, AE.at[0], in_sem.at[0]),
            pltpu.make_async_copy(eps_in, eps, in_sem.at[1]),
            pltpu.make_async_copy(e_in, E.at[0, :, 1:nx + 1, top:end, :], in_sem.at[2]),
            pltpu.make_async_copy(h_in, H.at[0, :, 1:nx + 1, top:end, :], in_sem.at[3]),
            pltpu.make_async_copy(ch_in, AH.at[0, :, 1:nx + 1, top:end, :], in_sem.at[4]),
            pltpu.make_async_copy(ids_in, ids, in_sem.at[5]),
        ]
        for j in (2, 3, 0, 1, 4, 5):
            loads[j].start()

        barrier = pltpu.get_barrier_semaphore()

        @pl.loop(1, n)
        def _(j):
            other = (me + j) % n
            pl.semaphore_signal(barrier, inc=1, device_id=(other // nb, other % nb), device_id_type=MESH)

        first_x, last_x = blk == 0, blk == nb - 1
        first_z, last_z = grp == 0, grp == ng - 1
        rounds = 2 * steps - 1

        @pl.when(last_x)
        def _():
            E[0:steps, 1:3, nx + 1, top:end, :] = jnp.zeros((steps, 2, nz, ny), jnp.float32)
            G[:, 1:3, nx + 1, top:end, :] = jnp.zeros((steps - 1, 2, nz, ny), jnp.float32)

        @pl.when(first_x)
        def _():
            H[:, 1:3, 0, top:end, :] = jnp.zeros((steps + 1, 2, nz, ny), jnp.float32)
            AH[:, 1:3, 0, top:end, :] = jnp.zeros((steps, 2, nz, ny), jnp.float32)

        @pl.when(last_z)
        def _():
            zl_dn[...] = jnp.zeros_like(zl_dn)

        @pl.when(jnp.logical_or(last_z, first_x))
        def _():
            cl_a[...] = jnp.zeros_like(cl_a)

        @pl.when(jnp.logical_or(first_z, last_x))
        def _():
            cl_b[...] = jnp.zeros_like(cl_b)

        def remote(src, dst, sems, r, to):
            return pltpu.make_async_remote_copy(src, dst, sems[0].at[r], sems[1].at[r], device_id=to, device_id_type=MESH)

        def links(r, buf):
            yes_dn, yes_up = jnp.logical_not(first_x), jnp.logical_not(last_x)
            z_dn, z_up = jnp.logical_not(first_z), jnp.logical_not(last_z)
            both = jnp.logical_and
            return [
                (yes_dn, yes_up, remote(buf.at[1:3, 1, top:end, :], buf.at[1:3, nx + 1, top:end, :], xd, r, (grp, blk - 1))),
                (yes_up, yes_dn, remote(buf.at[:, nx, top:end, :], buf.at[:, 0, top:end, :], xu, r, (grp, blk + 1))),
                (z_dn, z_up, remote(zs_dn.at[r], zl_dn.at[r], zd, r, (grp - 1, blk))),
                (z_up, z_dn, remote(zs_up.at[r], zl_up.at[r], zu, r, (grp + 1, blk))),
                (both(z_dn, yes_up), both(z_up, yes_dn), remote(zs_dn.at[r, 0, nx - 1], cl_a.at[r], ca, r, (grp - 1, blk + 1))),
                (both(z_up, yes_dn), both(z_dn, yes_up), remote(zs_up.at[r, 2, 0], cl_b.at[r], cb, r, (grp + 1, blk - 1))),
            ]

        def start_links(r, buf, h0=None, part_of=slice(None)):
            jobs = [links(r, buf)[part_of], hlinks(r, h0) if h0 is not None else []]
            for sends, _, copy in jobs[0] + jobs[1]:
                used.append((sends, copy))
                pl.when(sends)(copy.start)

        def hlinks(r, h0):
            q = 0 if r == 0 else 1
            return [
                (jnp.logical_not(last_x), jnp.logical_not(first_x), remote(h0.at[1:3, nx, top:end, :], h0.at[1:3, 0, top:end, :], hx, q, (grp, blk + 1))),
                (jnp.logical_not(last_z), jnp.logical_not(first_z), remote(zs_h.at[q], zl_h.at[q], hz, q, (grp + 1, blk))),
            ]

        used = []

        def finish_links(r, buf, h0=None):
            jobs = links(r, buf) + (hlinks(r, h0) if h0 is not None else [])
            for _, gets, copy in jobs:
                pl.when(gets)(copy.wait_recv)
            for c in range(2):
                for i in range(nx):
                    buf[c, i + 1, end:end + 1, :] = zl_dn[r, c, i]
            buf[0, 0, end:end + 1, :] = cl_a[r]
            buf[2, nx + 1, top - 1:top, :] = cl_b[r]

            @pl.when(jnp.logical_not(first_z))
            def _():
                for c in range(3):
                    for i in range(nx):
                        buf[c, i + 1, top - 1:top, :] = zl_up[r, c, i]
                if h0 is not None:
                    for c in range(2):
                        for i in range(nx):
                            h0[c, i + 1, top - 1:top, :] = zl_h[0 if r == 0 else 1, c, i]

        def curl_f(buf, i):
            vx, vy, vz = (buf[c, i, 0:end, :] for c in range(3))

            def dy(v):
                return jnp.where(lane_h == ny - 1, 0.0, pltpu.roll(v, ny - 1, 1)) - v

            dxy, dxz = (buf[c, i + 1, 0:end, :] - v for c, v in ((1, vy), (2, vz)))
            dzx, dzy = (buf[c, i, 1:end + 1, :] - v for c, v in ((0, vx), (1, vy)))
            return dy(vz) - dzy, dzx - dxz, dxy - dy(vx)

        def curl_b(buf, i):
            vx, vy, vz = (buf[c, i, top:end, :] for c in range(3))

            def dy(v):
                return v - jnp.where(lane == 0, 0.0, pltpu.roll(v, 1, 1))

            dxy, dxz = (v - buf[c, i - 1, top:end, :] for c, v in ((1, vy), (2, vz)))
            dzx, dzy = (v - buf[c, i, top - 1:end - 1, :] for c, v in ((0, vx), (1, vy)))
            return dy(vz) - dzy, dzx - dxz, dxy - dy(vx)

        def each(first, last, body):
            def step(i, carry):
                body(i)
                return carry
            lax.fori_loop(first, last, step, 0, unroll=UNROLL)

        def f_step(src, prev, dst, sign):
            def body(i):
                cv = curl_f(src, i)
                for c in range(3):
                    dst[c, i, 0:end, :] = prev[c, i, 0:end, :] + sign * cv[c]

            @pl.when(jnp.logical_not(first_x))
            def _():
                vx, vy, vz = (src[c, 0, top:end, :] for c in range(3))

                def dy(v):
                    return jnp.where(lane == ny - 1, 0.0, pltpu.roll(v, ny - 1, 1)) - v

                cy = (src[0, 0, top + 1:end + 1, :] - vx) - (src[2, 1, top:end, :] - vz)
                cz = (src[1, 1, top:end, :] - vy) - dy(vx)
                dst[1, 0, top:end, :] = prev[1, 0, top:end, :] + sign * cy
                dst[2, 0, top:end, :] = prev[2, 0, top:end, :] + sign * cz

            each(1, nx + 1, body)

            @pl.when(first_z)
            def _():
                for c in range(2):
                    for i in range(1, nx + 1):
                        dst[c, i, top - 1:top, :] = jnp.zeros((1, ny), jnp.float32)

        def edge_rows(r, c, i, new):
            if c < 2:
                zs_dn[r, c, i - 1] = new[0:1, :]
            zs_up[r, c, i - 1] = new[nz - 1:nz, :]

        ra = steps
        loads[2].wait()
        for i in range(1, nx + 1):
            for c in range(3):
                edge_rows(0, c, i, E[0, c, i, top:end, :])
        loads[3].wait()
        for i in range(1, nx + 1):
            for c in range(2):
                zs_h[0, c, i - 1] = H[0, c, i, end - 1:end, :]
        pl.semaphore_wait(barrier, n - 1)
        start_links(0, E.at[0], H.at[0])
        loads[0].wait()
        loads[1].wait()

        def first_g(i):
            for c in range(3):
                g = eps[i - 1] * AE[0, c, i - 1]
                G[0, c, i, top:end, :] = g
                edge_rows(ra, c, i, g)

        each(1, nx + 1, first_g)
        loads[4].wait()
        for i in range(1, nx + 1):
            for c in range(2):
                zs_h[1, c, i - 1] = AH[0, c, i, end - 1:end, :]
        start_links(ra, G.at[0], AH.at[0])
        loads[5].wait()

        for k in range(steps):
            finish_links(k, E.at[k], H.at[0] if k == 0 else None)
            f_step(E.at[k], H.at[k], H.at[k + 1], -COURANT)
            if k == steps - 1:
                h_copy = pltpu.make_async_copy(H.at[steps, :, 1:nx + 1, top:end, :], h_out, out_sem.at[0])
                h_copy.start()

            def e_body(i, k=k):
                cv = curl_b(H.at[k + 1], i)
                scale = COURANT * eps[i - 1]
                for c in range(3):
                    CURL[k, c, i - 1] = cv[c]
                    new = E[k, c, i, top:end, :] + scale * cv[c]
                    E[k + 1, c, i, top:end, :] = new
                    if k < steps - 1:
                        edge_rows(k + 1, c, i, new)

            e_body(1)
            e_body(nx)
            if k < steps - 1:
                start_links(k + 1, E.at[k + 1], part_of=slice(0, 2))
            each(2, nx, e_body)
            if k == steps - 1:
                e_copy = pltpu.make_async_copy(E.at[steps, :, 1:nx + 1, top:end, :], e_out, out_sem.at[1])
                e_copy.start()
                continue
            start_links(k + 1, E.at[k + 1], part_of=slice(2, 6))
            finish_links(ra + k, G.at[k], AH.at[0] if k == 0 else None)
            f_step(G.at[k], AH.at[k], AH.at[k + 1], COURANT)

            def a_body(i, k=k):
                cv = curl_b(AH.at[k + 1], i)
                for c in range(3):
                    new = AE[k, c, i - 1] - COURANT * cv[c]
                    AE[k + 1, c, i - 1] = new
                    if k < steps - 2:
                        g = eps[i - 1] * new
                        G[k + 1, c, i, top:end, :] = g
                        edge_rows(ra + k + 1, c, i, g)

            a_body(1)
            a_body(nx)
            if k < steps - 2:
                start_links(ra + k + 1, G.at[k + 1], part_of=slice(0, 2))
            each(2, nx, a_body)
            if k < steps - 2:
                start_links(ra + k + 1, G.at[k + 1], part_of=slice(2, 6))

        own = lax.broadcasted_iota(jnp.int32, (n, ny), 0)
        place = lax.broadcasted_iota(jnp.int32, (VOX_DEV, ny), 0)
        part[...] = jnp.zeros_like(part)

        def seg(i):
            grad = jnp.zeros((nz, ny), jnp.float32)
            for k in range(steps):
                for c in range(3):
                    grad = grad + AE[steps - 1 - k, c, i] * CURL[k, c, i]
            grad = COURANT * grad
            coarse = grad.astype(jnp.bfloat16).astype(jnp.float32)
            fine = grad - coarse
            v = ids[i]
            high, low = v // VOX_DEV, v % VOX_DEV
            lhs, rhs = [], []
            for z in range(nz):
                hit = high[z:z + 1, :] == own
                lhs.append(jnp.concatenate([
                    jnp.where(hit, coarse[z:z + 1, :], 0.0).astype(jnp.bfloat16),
                    jnp.where(hit, fine[z:z + 1, :], 0.0).astype(jnp.bfloat16)], axis=0))
                rhs.append(jnp.where(low[z:z + 1, :] == place, 1.0, 0.0).astype(jnp.bfloat16))
            part[...] += lax.dot_general(
                jnp.concatenate(lhs, axis=1), jnp.concatenate(rhs, axis=1),
                (((1,), (1,)), ((), ())), preferred_element_type=jnp.float32)

        lax.fori_loop(0, nx, lambda i, carry: (seg(i), carry)[1], 0, unroll=UNROLL)

        both = part[0:n, :] + part[n:2 * n, :]
        both = jnp.concatenate([both, jnp.zeros((n, 128 - VOX_DEV), jnp.float32)], axis=1)
        for d in range(n):
            S[d] = both[d:d + 1, :]

        @pl.loop(1, n)
        def _(j):
            to = (me + j) % n
            pltpu.make_async_remote_copy(
                S.at[to], R.at[me], as_sem, ar_sem,
                device_id=(to // nb, to % nb), device_id_type=MESH).start()

        R[me] = S[me]
        rest = pl.ds(0, n - 1)
        pltpu.make_async_copy(R.at[rest], R.at[rest], ar_sem).wait()
        v_out[...] = jnp.sum(R[...], axis=0)[:, 0:VOX_DEV]
        pltpu.make_async_copy(S.at[rest], S.at[rest], as_sem).wait()
        h_copy.wait()
        e_copy.wait()
        for sends, copy in used:
            pl.when(sends)(copy.wait_send)

    return kernel


def solution(mesh):
    ng, nb = mesh.shape["grp"], mesh.shape["blk"]
    n = ng * nb

    def local(e_field, h_field, inv_eps, cot_e, cot_h, voxel_ids):
        _, nx, nz, ny = e_field.shape
        f32 = jnp.float32
        padded = (3, nx + 2, nz + 16, ny)
        plain = (3, nx, nz, ny)
        rounds = 2 * STEPS - 1
        dma = pltpu.SemaphoreType.DMA
        hbm = pl.BlockSpec(memory_space=pl.ANY)
        e_new, h_new, vox = pl.pallas_call(
            make_kernel(ng, nb, nx, nz, ny),
            out_shape=(
                jax.ShapeDtypeStruct(plain, f32),
                jax.ShapeDtypeStruct(plain, f32),
                jax.ShapeDtypeStruct((1, VOX_DEV), f32),
            ),
            in_specs=[hbm] * 6,
            out_specs=(hbm, hbm, pl.BlockSpec(memory_space=pltpu.VMEM)),
            scratch_shapes=[
                pltpu.VMEM((STEPS + 1,) + padded, f32),
                pltpu.VMEM((STEPS + 1,) + padded, f32),
                pltpu.VMEM((STEPS - 1,) + padded, f32),
                pltpu.VMEM((STEPS,) + padded, f32),
                pltpu.VMEM((STEPS,) + plain, f32),
                pltpu.VMEM((STEPS,) + plain, f32),
                pltpu.VMEM(plain[1:], f32),
                pltpu.VMEM(plain[1:], jnp.int32),
                pltpu.VMEM((rounds, 2, nx, 1, ny), f32),
                pltpu.VMEM((rounds, 2, nx, 1, ny), f32),
                pltpu.VMEM((rounds, 3, nx, 1, ny), f32),
                pltpu.VMEM((rounds, 3, nx, 1, ny), f32),
                pltpu.VMEM((rounds, 1, ny), f32),
                pltpu.VMEM((rounds, 1, ny), f32),
                pltpu.VMEM((2, 2, nx, 1, ny), f32),
                pltpu.VMEM((2, 2, nx, 1, ny), f32),
                pltpu.VMEM((n, 1, 128), f32),
                pltpu.VMEM((n, 1, 128), f32),
                pltpu.VMEM((2 * n, VOX_DEV), f32),
                dma((6,)), dma((2,)), dma, dma,
            ] + [dma((rounds,))] * 12 + [dma((2,))] * 4,
            compiler_params=pltpu.CompilerParams(
                collective_id=0, has_side_effects=True, vmem_limit_bytes=60 * 1024 * 1024),
        )(e_field, h_field, inv_eps, cot_e, cot_h, voxel_ids)
        return e_new, h_new, vox.reshape(VOX_DEV)

    field, cell = P(None, "blk", "grp", None), P("blk", "grp", None)
    return jax.shard_map(
        local, mesh=mesh,
        in_specs=(field, field, cell, field, field, cell),
        out_specs=(field, field, P(("grp", "blk"))),
        check_vma=False,
    )
```

```python
import jax
import jax.numpy as jnp
from jax import lax
from jax.experimental import pallas as pl
from jax.experimental.pallas import tpu as pltpu
from jax.sharding import PartitionSpec as P

STEPS = 4
COURANT = 0.5
MESH = pl.DeviceIdType.MESH
VOX_DEV = 64
UNROLL = True


def make_kernel(ng, nb, nx, nz, ny):
    n = ng * nb
    steps = STEPS
    top, end = 8, 8 + nz

    def kernel(e_in, h_in, eps_in, ce_in, ch_in, ids_in, e_out, h_out, v_out,
               E, H, G, AH, AE, CURL, eps, ids, zs_dn, zl_dn, zs_up, zl_up, cl_a, cl_b, zs_h, zl_h,
               S, R, part, in_sem, out_sem, as_sem, ar_sem, *link_sems):
        xd, xu, zd, zu, ca, cb, hx, hz = (link_sems[2 * j:2 * j + 2] for j in range(8))
        grp = lax.axis_index("grp")
        blk = lax.axis_index("blk")
        me = grp * nb + blk
        lane = lax.broadcasted_iota(jnp.int32, (nz, ny), 1)
        lane_h = lax.broadcasted_iota(jnp.int32, (end, ny), 1)

        loads = [
            pltpu.make_async_copy(ce_in, AE.at[0], in_sem.at[0]),
            pltpu.make_async_copy(eps_in, eps, in_sem.at[1]),
            pltpu.make_async_copy(e_in, E.at[0, :, 1:nx + 1, top:end, :], in_sem.at[2]),
            pltpu.make_async_copy(h_in, H.at[0, :, 1:nx + 1, top:end, :], in_sem.at[3]),
            pltpu.make_async_copy(ch_in, AH.at[0, :, 1:nx + 1, top:end, :], in_sem.at[4]),
            pltpu.make_async_copy(ids_in, ids, in_sem.at[5]),
        ]
        for j in (2, 3, 0, 1, 4, 5):
            loads[j].start()

        barrier = pltpu.get_barrier_semaphore()

        @pl.loop(1, n)
        def _(j):
            other = (me + j) % n
            pl.semaphore_signal(barrier, inc=1, device_id=(other // nb, other % nb), device_id_type=MESH)

        first_x, last_x = blk == 0, blk == nb - 1
        first_z, last_z = grp == 0, grp == ng - 1
        rounds = 2 * steps - 1

        @pl.when(last_x)
        def _():
            E[0:steps, 1:3, nx + 1, top:end, :] = jnp.zeros((steps, 2, nz, ny), jnp.float32)
            G[:, 1:3, nx + 1, top:end, :] = jnp.zeros((steps - 1, 2, nz, ny), jnp.float32)

        @pl.when(first_x)
        def _():
            H[:, 1:3, 0, top:end, :] = jnp.zeros((steps + 1, 2, nz, ny), jnp.float32)
            AH[:, 1:3, 0, top:end, :] = jnp.zeros((steps, 2, nz, ny), jnp.float32)

        @pl.when(last_z)
        def _():
            zl_dn[...] = jnp.zeros_like(zl_dn)

        @pl.when(jnp.logical_or(last_z, first_x))
        def _():
            cl_a[...] = jnp.zeros_like(cl_a)

        @pl.when(jnp.logical_or(first_z, last_x))
        def _():
            cl_b[...] = jnp.zeros_like(cl_b)

        def remote(src, dst, sems, r, to):
            return pltpu.make_async_remote_copy(src, dst, sems[0].at[r], sems[1].at[r], device_id=to, device_id_type=MESH)

        def links(r, buf):
            yes_dn, yes_up = jnp.logical_not(first_x), jnp.logical_not(last_x)
            z_dn, z_up = jnp.logical_not(first_z), jnp.logical_not(last_z)
            both = jnp.logical_and
            return [
                (yes_dn, yes_up, remote(buf.at[1:3, 1, top:end, :], buf.at[1:3, nx + 1, top:end, :], xd, r, (grp, blk - 1))),
                (yes_up, yes_dn, remote(buf.at[:, nx, top:end, :], buf.at[:, 0, top:end, :], xu, r, (grp, blk + 1))),
                (z_dn, z_up, remote(zs_dn.at[r], zl_dn.at[r], zd, r, (grp - 1, blk))),
                (z_up, z_dn, remote(zs_up.at[r], zl_up.at[r], zu, r, (grp + 1, blk))),
                (both(z_dn, yes_up), both(z_up, yes_dn), remote(zs_dn.at[r, 0, nx - 1], cl_a.at[r], ca, r, (grp - 1, blk + 1))),
                (both(z_up, yes_dn), both(z_dn, yes_up), remote(zs_up.at[r, 2, 0], cl_b.at[r], cb, r, (grp + 1, blk - 1))),
            ]

        def start_links(r, buf, h0=None, part_of=slice(None)):
            jobs = [links(r, buf)[part_of], hlinks(r, h0) if h0 is not None else []]
            for sends, _, copy in jobs[0] + jobs[1]:
                used.append((sends, copy))
                pl.when(sends)(copy.start)

        def hlinks(r, h0):
            q = 0 if r == 0 else 1
            return [
                (jnp.logical_not(last_x), jnp.logical_not(first_x), remote(h0.at[1:3, nx, top:end, :], h0.at[1:3, 0, top:end, :], hx, q, (grp, blk + 1))),
                (jnp.logical_not(last_z), jnp.logical_not(first_z), remote(zs_h.at[q], zl_h.at[q], hz, q, (grp + 1, blk))),
            ]

        used = []

        def finish_links(r, buf, h0=None):
            jobs = links(r, buf) + (hlinks(r, h0) if h0 is not None else [])
            for _, gets, copy in jobs:
                pl.when(gets)(copy.wait_recv)
            for c in range(2):
                for i in range(nx):
                    buf[c, i + 1, end:end + 1, :] = zl_dn[r, c, i]
            buf[0, 0, end:end + 1, :] = cl_a[r]
            buf[2, nx + 1, top - 1:top, :] = cl_b[r]

            @pl.when(jnp.logical_not(first_z))
            def _():
                for c in range(3):
                    for i in range(nx):
                        buf[c, i + 1, top - 1:top, :] = zl_up[r, c, i]
                if h0 is not None:
                    for c in range(2):
                        for i in range(nx):
                            h0[c, i + 1, top - 1:top, :] = zl_h[0 if r == 0 else 1, c, i]

        def curl_f(buf, i):
            vx, vy, vz = (buf[c, i, 0:end, :] for c in range(3))

            def dy(v):
                return jnp.where(lane_h == ny - 1, 0.0, pltpu.roll(v, ny - 1, 1)) - v

            dxy, dxz = (buf[c, i + 1, 0:end, :] - v for c, v in ((1, vy), (2, vz)))
            dzx, dzy = (buf[c, i, 1:end + 1, :] - v for c, v in ((0, vx), (1, vy)))
            return dy(vz) - dzy, dzx - dxz, dxy - dy(vx)

        def curl_b(buf, i):
            vx, vy, vz = (buf[c, i, top:end, :] for c in range(3))

            def dy(v):
                return v - jnp.where(lane == 0, 0.0, pltpu.roll(v, 1, 1))

            dxy, dxz = (v - buf[c, i - 1, top:end, :] for c, v in ((1, vy), (2, vz)))
            dzx, dzy = (v - buf[c, i, top - 1:end - 1, :] for c, v in ((0, vx), (1, vy)))
            return dy(vz) - dzy, dzx - dxz, dxy - dy(vx)

        def each(first, last, body):
            def step(i, carry):
                body(i)
                return carry
            lax.fori_loop(first, last, step, 0, unroll=UNROLL)

        def f_step(src, prev, dst, sign):
            def body(i):
                cv = curl_f(src, i)
                for c in range(3):
                    dst[c, i, 0:end, :] = prev[c, i, 0:end, :] + sign * cv[c]

            @pl.when(jnp.logical_not(first_x))
            def _():
                vx, vy, vz = (src[c, 0, top:end, :] for c in range(3))

                def dy(v):
                    return jnp.where(lane == ny - 1, 0.0, pltpu.roll(v, ny - 1, 1)) - v

                cy = (src[0, 0, top + 1:end + 1, :] - vx) - (src[2, 1, top:end, :] - vz)
                cz = (src[1, 1, top:end, :] - vy) - dy(vx)
                dst[1, 0, top:end, :] = prev[1, 0, top:end, :] + sign * cy
                dst[2, 0, top:end, :] = prev[2, 0, top:end, :] + sign * cz

            each(1, nx + 1, body)

            @pl.when(first_z)
            def _():
                for c in range(2):
                    for i in range(1, nx + 1):
                        dst[c, i, top - 1:top, :] = jnp.zeros((1, ny), jnp.float32)

        def edge_rows(r, c, i, new):
            if c < 2:
                zs_dn[r, c, i - 1] = new[0:1, :]
            zs_up[r, c, i - 1] = new[nz - 1:nz, :]

        ra = steps
        loads[2].wait()
        for i in range(1, nx + 1):
            for c in range(3):
                edge_rows(0, c, i, E[0, c, i, top:end, :])
        loads[3].wait()
        for i in range(1, nx + 1):
            for c in range(2):
                zs_h[0, c, i - 1] = H[0, c, i, end - 1:end, :]
        pl.semaphore_wait(barrier, n - 1)
        start_links(0, E.at[0], H.at[0])
        loads[0].wait()
        loads[1].wait()

        def first_g(i):
            for c in range(3):
                g = eps[i - 1] * AE[0, c, i - 1]
                G[0, c, i, top:end, :] = g
                edge_rows(ra, c, i, g)

        each(1, nx + 1, first_g)
        loads[4].wait()
        for i in range(1, nx + 1):
            for c in range(2):
                zs_h[1, c, i - 1] = AH[0, c, i, end - 1:end, :]
        start_links(ra, G.at[0], AH.at[0])
        loads[5].wait()

        for k in range(steps):
            finish_links(k, E.at[k], H.at[0] if k == 0 else None)
            f_step(E.at[k], H.at[k], H.at[k + 1], -COURANT)
            if k == steps - 1:
                h_copy = pltpu.make_async_copy(H.at[steps, :, 1:nx + 1, top:end, :], h_out, out_sem.at[0])
                h_copy.start()

            def e_body(i, k=k):
                cv = curl_b(H.at[k + 1], i)
                scale = COURANT * eps[i - 1]
                for c in range(3):
                    CURL[k, c, i - 1] = cv[c]
                    new = E[k, c, i, top:end, :] + scale * cv[c]
                    E[k + 1, c, i, top:end, :] = new
                    if k < steps - 1:
                        edge_rows(k + 1, c, i, new)

            e_body(1)
            e_body(nx)
            if k < steps - 1:
                start_links(k + 1, E.at[k + 1], part_of=slice(0, 2))
            each(2, nx, e_body)
            if k == steps - 1:
                e_copy = pltpu.make_async_copy(E.at[steps, :, 1:nx + 1, top:end, :], e_out, out_sem.at[1])
                e_copy.start()
                continue
            start_links(k + 1, E.at[k + 1], part_of=slice(2, 6))
            finish_links(ra + k, G.at[k], AH.at[0] if k == 0 else None)
            f_step(G.at[k], AH.at[k], AH.at[k + 1], COURANT)

            def a_body(i, k=k):
                cv = curl_b(AH.at[k + 1], i)
                for c in range(3):
                    new = AE[k, c, i - 1] - COURANT * cv[c]
                    AE[k + 1, c, i - 1] = new
                    if k < steps - 2:
                        g = eps[i - 1] * new
                        G[k + 1, c, i, top:end, :] = g
                        edge_rows(ra + k + 1, c, i, g)

            a_body(1)
            a_body(nx)
            if k < steps - 2:
                start_links(ra + k + 1, G.at[k + 1], part_of=slice(0, 2))
            each(2, nx, a_body)
            if k < steps - 2:
                start_links(ra + k + 1, G.at[k + 1], part_of=slice(2, 6))

        own = lax.broadcasted_iota(jnp.int32, (n, ny), 0)
        place = lax.broadcasted_iota(jnp.int32, (VOX_DEV, ny), 0)
        part[...] = jnp.zeros_like(part)

        def seg(i):
            grad = jnp.zeros((nz, ny), jnp.float32)
            for k in range(steps):
                for c in range(3):
                    grad = grad + AE[steps - 1 - k, c, i] * CURL[k, c, i]
            grad = COURANT * grad
            coarse = grad.astype(jnp.bfloat16).astype(jnp.float32)
            fine = grad - coarse
            v = ids[i]
            high, low = v // VOX_DEV, v % VOX_DEV
            lhs, rhs = [], []
            for z in range(nz):
                hit = high[z:z + 1, :] == own
                lhs.append(jnp.concatenate([
                    jnp.where(hit, coarse[z:z + 1, :], 0.0).astype(jnp.bfloat16),
                    jnp.where(hit, fine[z:z + 1, :], 0.0).astype(jnp.bfloat16)], axis=0))
                rhs.append(jnp.where(low[z:z + 1, :] == place, 1.0, 0.0).astype(jnp.bfloat16))
            part[...] += lax.dot_general(
                jnp.concatenate(lhs, axis=1), jnp.concatenate(rhs, axis=1),
                (((1,), (1,)), ((), ())), preferred_element_type=jnp.float32)

        lax.fori_loop(0, nx, lambda i, carry: (seg(i), carry)[1], 0, unroll=UNROLL)

        both = part[0:n, :] + part[n:2 * n, :]
        both = jnp.concatenate([both, jnp.zeros((n, 128 - VOX_DEV), jnp.float32)], axis=1)
        for d in range(n):
            S[d] = both[d:d + 1, :]

        for dg in range(ng):
            to_grp = (grp + dg) % ng

            def send_row(db, carry, to_grp=to_grp):
                to_blk = (blk + db) % nb
                pltpu.make_async_remote_copy(
                    S.at[to_grp * nb + to_blk], R.at[me], as_sem, ar_sem,
                    device_id=(to_grp, to_blk), device_id_type=MESH).start()
                return carry

            lax.fori_loop(0 if dg else 1, nb, send_row, 0, unroll=True)

        R[me] = S[me]
        rest = pl.ds(0, n - 1)
        pltpu.make_async_copy(R.at[rest], R.at[rest], ar_sem).wait()
        v_out[...] = jnp.sum(R[...], axis=0)[:, 0:VOX_DEV]
        pltpu.make_async_copy(S.at[rest], S.at[rest], as_sem).wait()
        h_copy.wait()
        e_copy.wait()
        for sends, copy in used:
            pl.when(sends)(copy.wait_send)

    return kernel


def solution(mesh):
    ng, nb = mesh.shape["grp"], mesh.shape["blk"]
    n = ng * nb

    def local(e_field, h_field, inv_eps, cot_e, cot_h, voxel_ids):
        _, nx, nz, ny = e_field.shape
        f32 = jnp.float32
        padded = (3, nx + 2, nz + 16, ny)
        plain = (3, nx, nz, ny)
        rounds = 2 * STEPS - 1
        dma = pltpu.SemaphoreType.DMA
        hbm = pl.BlockSpec(memory_space=pl.ANY)
        e_new, h_new, vox = pl.pallas_call(
            make_kernel(ng, nb, nx, nz, ny),
            out_shape=(
                jax.ShapeDtypeStruct(plain, f32),
                jax.ShapeDtypeStruct(plain, f32),
                jax.ShapeDtypeStruct((1, VOX_DEV), f32),
            ),
            in_specs=[hbm] * 6,
            out_specs=(hbm, hbm, pl.BlockSpec(memory_space=pltpu.VMEM)),
            scratch_shapes=[
                pltpu.VMEM((STEPS + 1,) + padded, f32),
                pltpu.VMEM((STEPS + 1,) + padded, f32),
                pltpu.VMEM((STEPS - 1,) + padded, f32),
                pltpu.VMEM((STEPS,) + padded, f32),
                pltpu.VMEM((STEPS,) + plain, f32),
                pltpu.VMEM((STEPS,) + plain, f32),
                pltpu.VMEM(plain[1:], f32),
                pltpu.VMEM(plain[1:], jnp.int32),
                pltpu.VMEM((rounds, 2, nx, 1, ny), f32),
                pltpu.VMEM((rounds, 2, nx, 1, ny), f32),
                pltpu.VMEM((rounds, 3, nx, 1, ny), f32),
                pltpu.VMEM((rounds, 3, nx, 1, ny), f32),
                pltpu.VMEM((rounds, 1, ny), f32),
                pltpu.VMEM((rounds, 1, ny), f32),
                pltpu.VMEM((2, 2, nx, 1, ny), f32),
                pltpu.VMEM((2, 2, nx, 1, ny), f32),
                pltpu.VMEM((n, 1, 128), f32),
                pltpu.VMEM((n, 1, 128), f32),
                pltpu.VMEM((2 * n, VOX_DEV), f32),
                dma((6,)), dma((2,)), dma, dma,
            ] + [dma((rounds,))] * 12 + [dma((2,))] * 4,
            compiler_params=pltpu.CompilerParams(
                collective_id=0, has_side_effects=True, vmem_limit_bytes=60 * 1024 * 1024),
        )(e_field, h_field, inv_eps, cot_e, cot_h, voxel_ids)
        return e_new, h_new, vox.reshape(VOX_DEV)

    field, cell = P(None, "blk", "grp", None), P("blk", "grp", None)
    return jax.shard_map(
        local, mesh=mesh,
        in_specs=(field, field, cell, field, field, cell),
        out_specs=(field, field, P(("grp", "blk"))),
        check_vma=False,
    )
```
